32 devices in a mesh: groups: 2 (over x), tile: 16 (over z, y, core).
Axes of the slice: x: 2, y: 2, z: 4, core: 2. Of those that a mesh axis runs over, the one named last changes fastest.
Arguments:
- features: bfloat16 [128, 8, 16, 512], P(('groups', 'tile')), parts along dimension 0, may hold values from -80 to 80
- owner_frames: int32 [8], P('groups'), parts along dimension 0, may hold values from 2 to 4, as said below
- video_frames: int32 [8], P('groups'), parts along dimension 0, may hold values from 1 to 7, 12 in all
- first_gain: float32 [512], replicated, may hold values from 0.5 to 1.5
- first_shift: float32 [512], replicated, may hold values from -3 to 3
- first_kernel: bfloat16 [3, 3, 3, 512, 256], replicated, may hold values from -0.0546875 to 0.0546875
- first_bias: float32 [256], replicated, may hold values from -3 to 3
- second_gain: float32 [256], replicated, may hold values from 0.5 to 1.5
- second_shift: float32 [256], replicated, may hold values from -3 to 3
- second_kernel: bfloat16 [3, 3, 3, 256, 256], replicated, may hold values from -0.078125 to 0.078125
- second_bias: float32 [256], replicated, may hold values from -3 to 3
- skip_kernel: bfloat16 [512, 256], replicated, may hold values from -0.25 to 0.25
- skip_bias: float32 [256], replicated, may hold values from -3 to 3
Outputs:
- decoded_slots: bfloat16 [128, 8, 16, 256], P(('groups', 'tile')), parts along dimension 0
The draws below stay inside these ranges and needn't reach their ends.
There are 2 independent parts, one for each index of `groups`. The reference program is written for one: setup_inputs(seed, part) draws one part's arguments, and reference() takes and returns one part's arrays. A program takes and returns all parts, laid end to end along the dimension named above; an argument that names none is the same for every part. Nothing has to cross between parts.
Inputs may be any that keep to these rules, and one draw needn't show every extreme that they name: `owner_frames`: owner o holds the consecutive frames that follow all frames of the owners before it; the counts sum to 12; some owner holds 4 frames and some holds 2. `video_frames`: videos follow one another along the frames in order; the counts sum to 12.
All inputs are finite; a program needn't handle non-finite values.
Results may differ from the reference program's by a relative error of at most 0.003.
Values may be sent and summed in bfloat16 or wider, within the bound.
A program may use at most 64 MiB of HBM per device.

```python
import math
import jax
import jax.numpy as jnp
import numpy as np
from jax import lax

C_IN = 512
C_OUT = 256
GROUPS_N = 32
STRIPS = 4
CAP = 4
ROWS = 8
COLS = 16
OWNERS = 4
HEIGHT = 32
FRAMES = 12
VIDEOS = 4
LONGEST = 7


def draw_features(key, part):
    key_noise, key_pixel, key_channel = jax.random.split(key, 3)
    blocks = OWNERS * STRIPS * CAP
    shape = (blocks, ROWS, COLS, C_IN)
    block_ids = (jnp.arange(blocks, dtype=jnp.int32) // CAP).astype(jnp.float32)
    rising = jnp.exp(jnp.log(3.0) * (block_ids / max(OWNERS * STRIPS - 1, 1) - 0.5))
    noise = jnp.clip(jax.random.normal(key_noise, shape, jnp.float32), -4.0, 4.0)
    pixel_scale = jnp.exp(jax.random.uniform(key_pixel, (blocks, ROWS, COLS, 1), jnp.float32, jnp.log(0.3), jnp.log(3.0)))
    channel_scale = jnp.exp(jax.random.uniform(key_channel, (C_IN,), jnp.float32, jnp.log(0.3), jnp.log(3.0)))
    values = noise * pixel_scale * channel_scale * rising[:, None, None, None]
    return values.astype(jnp.bfloat16)


def draw_owner_frames(key, part):
    key_rank, key_count = jax.random.split(jax.random.fold_in(key, 71), 2)
    ranks = jax.random.permutation(key_rank, OWNERS).astype(jnp.int32)
    pairs = jax.random.randint(key_count, (), 1, OWNERS // 2 + 1).astype(jnp.int32)
    raised = (ranks < pairs).astype(jnp.int32)
    lowered = ((ranks >= pairs) & (ranks < 2 * pairs)).astype(jnp.int32)
    return (3 + raised - lowered).astype(jnp.int32)


def split_up(amount, total, bound, lean):
    loads = [(1 << 20) // math.isqrt(grade ** lean) + 1 for grade in range(2, amount + 1)]
    surplus, holding = total - bound - (amount - 1), [1] * (amount - 1)
    while surplus > 0:
        movable = [i for i in range(amount - 1) if holding[i] < bound]
        pool, left = sum([loads[i] for i in movable]), surplus
        for i in movable:
            addition = min(bound - holding[i], max(1, left * loads[i] // pool), surplus)
            holding[i] = holding[i] + addition
            surplus = surplus - addition
    return np.array([bound] + holding)


def uneven_parts(rng, number_of, total, most, lean):
    if number_of == 2:
        one = jax.random.randint(rng, (), max(1, total - most), min(most, total - 1) + 1)
        return jnp.stack([one, total - one])
    tallies = jnp.asarray(split_up(number_of, total, most, lean), jnp.int32)
    couples = (number_of - 1) // 2
    source_of, taker = tallies[1:1 + 2 * couples:2], tallies[2:2 + 2 * couples:2]
    room = jnp.minimum(source_of - 1, most - taker)
    moved = jax.random.randint(jax.random.fold_in(rng, 1), (couples,), 0, 1 << 20) % (room + 1)
    tallies = tallies.at[1:1 + 2 * couples:2].set(source_of - moved).at[2:2 + 2 * couples:2].set(taker + moved)
    return tallies[jax.random.permutation(jax.random.fold_in(rng, 2), number_of)]


def scatter_about(key, dims, scale, reach, held_as=jnp.bfloat16):
    entries = jax.random.normal(key, dims, jnp.float32) * scale
    return jnp.minimum(jnp.maximum(entries, -reach), reach).astype(held_as)


def setup_inputs(seed: int = 0, part: int = 0) -> dict:
    keys = jax.random.split(jax.random.key(seed), 14)
    part_splits = jax.random.split(jax.random.fold_in(keys[13], part), 14)
    return {
        "features": draw_features(jax.random.fold_in(jax.random.fold_in(keys[13], part), 71), part),
        "owner_frames": draw_owner_frames(jax.random.fold_in(jax.random.fold_in(keys[13], part), 71), part),
        "video_frames": uneven_parts(part_splits[2], VIDEOS, FRAMES, LONGEST, 1).astype(jnp.int32),
        "first_gain": jnp.clip(jax.random.uniform(keys[3], (C_IN,), jnp.float32, 0.5, 1.5), 0.5, 1.5),
        "first_shift": scatter_about(keys[4], (C_IN,), 0.5, 3.0, jnp.float32),
        "first_kernel": scatter_about(keys[5], (3, 3, 3, C_IN, C_OUT), (27 * C_IN) ** -0.5, 0.0546875),
        "first_bias": scatter_about(keys[6], (C_OUT,), 0.5, 3.0, jnp.float32),
        "second_gain": jnp.clip(jax.random.uniform(keys[7], (C_OUT,), jnp.float32, 0.5, 1.5), 0.5, 1.5),
        "second_shift": scatter_about(keys[8], (C_OUT,), 0.5, 3.0, jnp.float32),
        "second_kernel": scatter_about(keys[9], (3, 3, 3, C_OUT, C_OUT), (27 * C_OUT) ** -0.5, 0.078125),
        "second_bias": scatter_about(keys[10], (C_OUT,), 0.5, 3.0, jnp.float32),
        "skip_kernel": scatter_about(keys[11], (C_IN, C_OUT), C_IN ** -0.5, 0.25),
        "skip_bias": scatter_about(keys[12], (C_OUT,), 0.5, 3.0, jnp.float32),
    }


norm_eps = 1e-06
highest = lax.Precision.HIGHEST

def frame_layout(owner_frames, video_frames):
    owner_end = jnp.cumsum(owner_frames).astype(jnp.int32)
    owner_begin = (owner_end - owner_frames).astype(jnp.int32)
    video_end = jnp.cumsum(video_frames).astype(jnp.int32)
    video_begin = (video_end - video_frames).astype(jnp.int32)
    frame_ids = jnp.arange(FRAMES, dtype=jnp.int32)
    owner_ids = jnp.arange(OWNERS, dtype=jnp.int32)
    owner_of = lax.optimization_barrier(jnp.sum((owner_end[None, :] <= frame_ids[:, None]).astype(jnp.int32), axis=1)).astype(jnp.int32)
    owner_match = owner_ids[None, :] == owner_of[:, None]
    owner_first = lax.optimization_barrier(jnp.sum(jnp.where(owner_match, owner_begin[None, :], 0), axis=1)).astype(jnp.int32)
    stored_row = (owner_of * CAP + frame_ids - owner_first).astype(jnp.int32)
    inside = (frame_ids[:, None] >= video_begin[None, :]) & (frame_ids[:, None] < video_end[None, :])
    video_first = lax.optimization_barrier(jnp.sum(jnp.where(inside, video_begin[None, :], 0), axis=1)).astype(jnp.int32)
    prior_table = jnp.stack([jnp.maximum(frame_ids - 2 + time_tap, video_first) for time_tap in range(3)], axis=1).astype(jnp.int32)
    return (stored_row, inside.astype(jnp.float32), prior_table, owner_begin)

def group_activate(values, member, video_frames, gain, shift_vec):
    frames, height, width, channels = values.shape
    group_width = channels // GROUPS_N
    widened = values.astype(jnp.float32)
    cell_counts = (video_frames * (height * width * group_width)).astype(jnp.float32)
    slot_sums = lax.optimization_barrier(jnp.sum(widened, axis=(1, 2))).reshape(frames, GROUPS_N, group_width).sum(axis=2)
    mean_table = jnp.dot(member.T, slot_sums, precision=highest) / cell_counts[:, None]
    centre = jnp.repeat(jnp.dot(member, mean_table, precision=highest), group_width, axis=1)
    centred = widened - centre[:, None, None, :]
    squares = lax.optimization_barrier(jnp.sum(centred * centred, axis=(1, 2))).reshape(frames, GROUPS_N, group_width).sum(axis=2)
    spread = jnp.dot(member.T, squares, precision=highest) / cell_counts[:, None]
    inverse_table = lax.rsqrt(spread + norm_eps)
    scaling = jnp.repeat(jnp.dot(member, inverse_table, precision=highest), group_width, axis=1)
    normed = centred * scaling[:, None, None, :] * gain + shift_vec
    return jax.nn.silu(normed).astype(jnp.bfloat16)

def causal_conv(acts, kernel, prior_table):
    frames, height, width, channels = acts.shape
    padded = jnp.pad(acts, ((0, 0), (1, 1), (1, 1), (0, 0)), mode='edge')
    running = jnp.zeros((frames * height * width, kernel.shape[-1]), jnp.float32)
    for time_tap in range(3):
        source = jnp.take(padded, prior_table[:, time_tap], axis=0)
        for row_tap in range(3):
            for col_tap in range(3):
                piece = source[:, row_tap:row_tap + height, col_tap:col_tap + width, :].reshape(-1, channels)
                running = running + jnp.dot(piece, kernel[time_tap, row_tap, col_tap], preferred_element_type=jnp.float32)
    return running.reshape(frames, height, width, -1)

def reference(features, owner_frames, video_frames, first_gain, first_shift, first_kernel, first_bias, second_gain, second_shift, second_kernel, second_bias, skip_kernel, skip_bias):
    lead = STRIPS + STRIPS // 2
    stored_row, member, prior_table, owner_begin = frame_layout(owner_frames, video_frames)
    by_device = features.reshape(OWNERS * STRIPS, CAP, ROWS, COLS, C_IN)
    by_position = jnp.roll(by_device, lead, axis=0)
    blocks = by_position.reshape(OWNERS, STRIPS, CAP, ROWS, COLS, C_IN).transpose(0, 2, 1, 3, 4, 5).reshape(OWNERS * CAP, HEIGHT, COLS, C_IN)
    inputs = jnp.take(blocks, stored_row, axis=0)
    first_acts = group_activate(inputs, member, video_frames, first_gain, first_shift)
    hidden = (causal_conv(first_acts, first_kernel, prior_table) + first_bias).astype(jnp.bfloat16)
    second_acts = group_activate(hidden, member, video_frames, second_gain, second_shift)
    mixed = causal_conv(second_acts, second_kernel, prior_table) + second_bias
    skipped = jnp.dot(inputs.reshape(-1, C_IN), skip_kernel, preferred_element_type=jnp.float32).reshape(FRAMES, HEIGHT, COLS, C_OUT) + skip_bias
    decoded = (mixed + skipped).astype(jnp.bfloat16)
    slot_ids = jnp.arange(OWNERS * CAP, dtype=jnp.int32)
    slot_owner = (slot_ids // CAP).astype(jnp.int32)
    slot_within = slot_ids - slot_owner * CAP
    owner_match = jnp.arange(OWNERS, dtype=jnp.int32)[None, :] == slot_owner[:, None]
    slot_count = lax.optimization_barrier(jnp.sum(jnp.where(owner_match, owner_frames[None, :], 0), axis=1))
    slot_begin = lax.optimization_barrier(jnp.sum(jnp.where(owner_match, owner_begin[None, :], 0), axis=1))
    live_slots = slot_within < slot_count
    frame_of = jnp.minimum(slot_begin + slot_within, FRAMES - 1).astype(jnp.int32)
    placed = jnp.where(live_slots[:, None, None, None], jnp.take(decoded, frame_of, axis=0), jnp.zeros((), jnp.bfloat16))
    placed = placed.reshape(OWNERS, CAP, STRIPS, ROWS, COLS, C_OUT).transpose(0, 2, 1, 3, 4, 5).reshape(OWNERS * STRIPS, CAP, ROWS, COLS, C_OUT)
    return jnp.roll(placed, -lead, axis=0).reshape(OWNERS * STRIPS * CAP, ROWS, COLS, C_OUT)
```

```python
import functools

import jax
import jax.numpy as jnp
from jax import lax
from jax.experimental import pallas as pl
from jax.experimental.pallas import tpu as pltpu
from jax.sharding import PartitionSpec as P

GROUPS_N = 32
STRIPS = 4
LANES = 128
EPS = 1e-06
HIGHEST = lax.Precision.HIGHEST
MESH = pl.DeviceIdType.MESH
F32 = jnp.float32
BF16 = jnp.bfloat16


def spread(channels, offset, transposed):
    width = channels // GROUPS_N
    shape = (LANES, channels) if transposed else (channels, LANES)
    chan = lax.broadcasted_iota(jnp.int32, shape, 1 if transposed else 0)
    lane = (lax.broadcasted_iota(jnp.int32, shape, 0 if transposed else 1) - offset) * width
    return jnp.where((chan >= lane) & (chan < lane + width), 1.0, 0.0).astype(F32)


def kernel(
    n,
    feat_hbm, owner_ref, video_ref, gain1, shift1, w1_hbm, bias1, gain2, shift2, w2_hbm, bias2, skip_hbm, bias3,
    out_ref,
    feat, w1, w2, skip,
    last1, prior1, up1, down1, act1, st1, gath1,
    hid, last2, prior2, up2, down2, act2, st2, gath2,
    acc, skipped,
    load_sem, w1_sem, w2_sem, halo_send, halo_recv, stat_send, stat_recv,
):
    me = lax.axis_index("tile")
    cap, rows, cols, c_in = feat.shape
    c_out = hid.shape[3]
    frames = cap + 2
    owners, videos = owner_ref.shape[0], video_ref.shape[0]
    cells = rows * cols
    height = rows * STRIPS
    vpad = st1.shape[0]

    def peer(by):
        return lax.rem(me + (by % n), n)

    barrier = pltpu.get_barrier_semaphore()

    def greet(d, carry):
        pl.semaphore_signal(barrier, inc=1, device_id={"tile": lax.rem(me + d, n)}, device_id_type=MESH)
        return carry

    load_feat = pltpu.make_async_copy(feat_hbm, feat, load_sem.at[0])
    load_feat.start()
    load_w1 = [pltpu.make_async_copy(w1_hbm.at[k], w1.at[k], w1_sem.at[k]) for k in range(3)]
    load_w2 = [pltpu.make_async_copy(w2_hbm.at[k], w2.at[k], w2_sem.at[k]) for k in range(3)]
    load_skip = pltpu.make_async_copy(skip_hbm, skip, load_sem.at[1])
    lax.fori_loop(1, n, greet, 0)
    for c in load_w1:
        c.start()
    load_skip.start()
    for c in load_w2:
        c.start()

    position = lax.rem(me + STRIPS + STRIPS // 2, n)
    owner = position // STRIPS
    strip = position - owner * STRIPS
    first = jnp.int32(0)
    live = jnp.int32(0)
    for o in range(owners):
        count = owner_ref[o]
        first = first + jnp.where(o < owner, count, 0)
        live = live + jnp.where(o == owner, count, 0)
    tail = jnp.minimum(jnp.maximum(live - 2, 0), cap - 2)
    begins = []
    total = jnp.int32(0)
    for v in range(videos):
        begins.append(total)
        total = total + video_ref[v]
    which, started, lengths = [], [], []
    for f in range(frames):
        t = first + (f - 2)
        row, start, length = jnp.int32(-1), jnp.int32(0), jnp.int32(1)
        for v in range(videos):
            count = video_ref[v]
            hit = (t >= begins[v]) & (t < begins[v] + count)
            row = jnp.where(hit, v, row)
            start = jnp.where(hit, begins[v], start)
            length = jnp.where(hit, count, length)
        which.append(row)
        started.append(start)
        lengths.append(length)

    def halo_copies(stage, source, last, prior, up, down):
        moves = (
            (source.at[:, rows - 1], up.at[pl.ds(2, cap)], 1),
            (source.at[:, 0], down.at[pl.ds(2, cap)], -1),
            (last.at[:, rows - 1], up.at[pl.ds(0, 2)], STRIPS + 1),
            (last.at[:, 0], down.at[pl.ds(0, 2)], STRIPS - 1),
            (last, prior, STRIPS),
        )
        return [
            pltpu.make_async_remote_copy(
                src_ref=src, dst_ref=dst, send_sem=halo_send.at[stage, i], recv_sem=halo_recv.at[stage, i],
                device_id={"tile": peer(by)}, device_id_type=MESH)
            for i, (src, dst, by) in enumerate(moves)
        ]

    def stat_copy(stage, d, st, gath):
        return pltpu.make_async_remote_copy(
            src_ref=st, dst_ref=gath.at[d], send_sem=stat_send.at[stage, d], recv_sem=stat_recv.at[stage, d],
            device_id={"tile": lax.rem(me + d, n)}, device_id_type=MESH)

    def send_stats(stage, st, gath):
        def one(d, carry):
            stat_copy(stage, d, st, gath).start()
            return carry
        lax.fori_loop(1, n, one, 0)

    def wait_stats(stage, st, gath):
        def one(d, carry):
            stat_copy(stage, d, st, gath).wait()
            return carry
        lax.fori_loop(1, n, one, 0)

    row_ids = lax.broadcasted_iota(jnp.int32, (vpad, LANES), 0)

    def local_stats(values, channels):
        sums, squares = [], []
        for j in range(cap):
            x = values(j)
            sums.append(jnp.sum(x, axis=0, keepdims=True))
            squares.append(jnp.sum(x * x, axis=0, keepdims=True))
        pad = [jnp.zeros((8 - cap, channels), F32)] if cap < 8 else []
        s = jnp.concatenate(sums + pad, axis=0)
        q = jnp.concatenate(squares + pad, axis=0)
        grouped = jnp.dot(s, spread(channels, 0, False), precision=HIGHEST, preferred_element_type=F32)
        grouped = grouped + jnp.dot(
            q, spread(channels, GROUPS_N, False), precision=HIGHEST, preferred_element_type=F32)
        table = jnp.zeros((vpad, LANES), F32)
        for j in range(cap):
            target = jnp.where(j < live, which[j + 2], -1)
            table = table + jnp.where(row_ids == target, grouped[j:j + 1, :], 0.0)
        return table

    def tables(st, gath, channels, gain, shift):
        totals = st[...]
        for d in range(1, n):
            totals = totals + gath[d]
        ids = lax.broadcasted_iota(jnp.int32, (8, LANES), 0)
        picked = jnp.zeros((8, LANES), F32)
        counts = jnp.ones((8, LANES), F32)
        for f in range(frames):
            mine = jnp.sum(jnp.where(row_ids == which[f], totals, 0.0), axis=0, keepdims=True)
            picked = jnp.where(ids == f, mine, picked)
            size = (lengths[f] * (height * cols * (channels // GROUPS_N))).astype(F32)
            counts = jnp.where(ids == f, size, counts)
        average = picked / counts
        mean = jnp.dot(average, spread(channels, 0, True), precision=HIGHEST, preferred_element_type=F32)
        square = jnp.dot(average, spread(channels, GROUPS_N, True), precision=HIGHEST, preferred_element_type=F32)
        inverse = lax.rsqrt(jnp.maximum(square - mean * mean, 0.0) + EPS)
        return mean, inverse * gain[...].reshape(1, channels), shift[...].reshape(1, channels)

    def activate(x, f, table):
        mean, scale, offset = table
        u = (x.astype(F32) - mean[f:f + 1]) * scale[f:f + 1] + offset
        return (u * (0.5 + 0.5 * jnp.tanh(0.5 * u))).astype(BF16)

    def fill(act, own, prior, up, down, table, channels):
        for f in range(frames):
            for r in range(rows):
                x = prior[f, r] if f < 2 else own[f - 2, r]
                act[f, r + 1] = activate(x, f, table)
            top = activate(up[f], f, table)
            act[f, 0] = jnp.where(strip == 0, act[f, 1], top)
            low = activate(down[f], f, table)
            act[f, rows + 1] = jnp.where(strip == STRIPS - 1, act[f, rows], low)

    def convolve(act, w, loads, channels):
        for k in range(3):
            loads[k].wait()

        acc[...] = jnp.zeros_like(acc)

        def step(it, carry):
            k = it // 3
            q = it - k * 3
            lhs = []
            for i in range(3):
                parts = []
                for j in range(cap):
                    f = jnp.minimum(jnp.maximum(j + k, started[j + 2] - first + 2), frames - 1)
                    parts.append(act[f, i:i + rows].reshape(cells, channels))
                lhs.append(jnp.concatenate(parts, axis=0))
            left = jnp.concatenate(lhs, axis=1)
            right = jnp.concatenate([w[k, i, q] for i in range(3)], axis=0)
            acc[q] += jnp.dot(left, right, preferred_element_type=F32)
            return carry

        lax.fori_loop(0, 9, step, 0)

    def joined(j):
        at = pl.ds(j * cells, cells)
        low, mid, high = acc[0, at], acc[1, at], acc[2, at]
        col = lax.rem(lax.broadcasted_iota(jnp.int32, low.shape, 0), cols)
        low = jnp.where(col == 0, low, pltpu.roll(low, 1, 0))
        high = jnp.where(col == cols - 1, high, pltpu.roll(high, cells - 1, 0))
        return low + mid + high

    load_feat.wait()
    last1[...] = feat[pl.ds(tail, 2)]
    st1[...] = local_stats(lambda j: feat[j].reshape(cells, c_in).astype(F32), c_in)
    pl.semaphore_wait(barrier, n - 1)
    halos = halo_copies(0, feat, last1, prior1, up1, down1)
    send_stats(0, st1, gath1)
    for c in halos:
        c.start()
    wait_stats(0, st1, gath1)
    table = tables(st1, gath1, c_in, gain1, shift1)
    for c in halos:
        c.wait()
    fill(act1, feat, prior1, up1, down1, table, c_in)
    convolve(act1, w1, load_w1, c_in)

    for j in range(cap):
        hid[j] = (joined(j) + bias1[...].reshape(1, c_out)).astype(BF16).reshape(rows, cols, c_out)
    last2[...] = hid[pl.ds(tail, 2)]
    st2[...] = local_stats(lambda j: hid[j].reshape(cells, c_out).astype(F32), c_out)
    halos = halo_copies(1, hid, last2, prior2, up2, down2)
    send_stats(1, st2, gath2)
    for c in halos:
        c.start()
    load_skip.wait()
    skipped[...] = jnp.dot(
        feat[...].reshape(cap * cells, c_in), skip[...], preferred_element_type=F32)
    wait_stats(1, st2, gath2)
    table = tables(st2, gath2, c_out, gain2, shift2)
    for c in halos:
        c.wait()
    fill(act2, hid, prior2, up2, down2, table, c_out)
    convolve(act2, w2, load_w2, c_out)
    extra = bias2[...].reshape(1, c_out) + bias3[...].reshape(1, c_out)
    for j in range(cap):
        value = joined(j) + skipped[pl.ds(j * cells, cells)] + extra
        value = jnp.where(j < live, value, 0.0)
        out_ref[j] = value.astype(BF16).reshape(rows, cols, c_out)


def on_device(n, features, owner_frames, video_frames, gain1, shift1, w1, bias1, gain2, shift2, w2, bias2, skip, bias3):
    cap, rows, cols, c_in = features.shape
    c_out = w1.shape[4]
    vpad = -(-video_frames.shape[0] // 8) * 8
    frames = cap + 2
    cells = rows * cols

    def buffers(channels):
        return [
            pltpu.VMEM((2, rows, cols, channels), BF16),
            pltpu.VMEM((2, rows, cols, channels), BF16),
            pltpu.VMEM((frames, cols, channels), BF16),
            pltpu.VMEM((frames, cols, channels), BF16),
            pltpu.VMEM((frames, rows + 2, cols, channels), BF16),
            pltpu.VMEM((vpad, LANES), F32),
            pltpu.VMEM((n, vpad, LANES), F32),
        ]

    hbm, vmem, smem = (pl.BlockSpec(memory_space=s) for s in (pl.ANY, pltpu.VMEM, pltpu.SMEM))
    return pl.pallas_call(
        functools.partial(kernel, n),
        out_shape=jax.ShapeDtypeStruct((cap, rows, cols, c_out), BF16),
        in_specs=[hbm, smem, smem, vmem, vmem, hbm, vmem, vmem, vmem, hbm, vmem, hbm, vmem],
        out_specs=vmem,
        scratch_shapes=[
            pltpu.VMEM(features.shape, BF16),
            pltpu.VMEM(w1.shape, BF16),
            pltpu.VMEM(w2.shape, BF16),
            pltpu.VMEM(skip.shape, BF16),
            *buffers(c_in),
            pltpu.VMEM((cap, rows, cols, c_out), BF16),
            *buffers(c_out),
            pltpu.VMEM((3, cap * cells, c_out), F32),
            pltpu.VMEM((cap * cells, c_out), F32),
            pltpu.SemaphoreType.DMA((2,)),
            pltpu.SemaphoreType.DMA((3,)),
            pltpu.SemaphoreType.DMA((3,)),
            pltpu.SemaphoreType.DMA((2, 5)),
            pltpu.SemaphoreType.DMA((2, 5)),
            pltpu.SemaphoreType.DMA((2, n)),
            pltpu.SemaphoreType.DMA((2, n)),
        ],
        compiler_params=pltpu.CompilerParams(
            collective_id=0, has_side_effects=True, vmem_limit_bytes=60 * 1024 * 1024),
    )(features, owner_frames, video_frames, gain1, shift1, w1, bias1, gain2, shift2, w2, bias2, skip, bias3)


def solution(mesh):
    split = P(("groups", "tile"), None, None, None)
    placed = (split, P("groups"), P("groups")) + (P(),) * 10
    return jax.shard_map(
        functools.partial(on_device, mesh.shape["tile"]),
        mesh=mesh,
        in_specs=placed,
        out_specs=split,
        check_vma=False,
    )
```

```python
import functools

import jax
import jax.numpy as jnp
from jax import lax
from jax.experimental import pallas as pl
from jax.experimental.pallas import tpu as pltpu
from jax.sharding import PartitionSpec as P

GROUPS_N = 32
STRIPS = 4
LANES = 128
EPS = 1e-06
HIGHEST = lax.Precision.HIGHEST
MESH = pl.DeviceIdType.MESH
F32 = jnp.float32
BF16 = jnp.bfloat16


def spread(channels, offset, transposed):
    width = channels // GROUPS_N
    shape = (LANES, channels) if transposed else (channels, LANES)
    chan = lax.broadcasted_iota(jnp.int32, shape, 1 if transposed else 0)
    lane = (lax.broadcasted_iota(jnp.int32, shape, 0 if transposed else 1) - offset) * width
    return jnp.where((chan >= lane) & (chan < lane + width), 1.0, 0.0).astype(F32)


def kernel(
    n,
    feat_hbm, owner_hbm, video_hbm, gain1_hbm, shift1_hbm, w1_hbm, bias1_hbm, gain2_hbm, shift2_hbm, w2_hbm, bias2_hbm,
    skip_hbm, bias3_hbm,
    out_ref,
    owner_ref, video_ref, gain1, shift1, bias1, gain2, shift2, bias2, bias3,
    feat, w1, w2, skip,
    last1, prior1, up1, down1, act1, st1, gath1,
    hid, last2, prior2, up2, down2, act2, st2, gath2,
    acc, skipped,
    load_sem, small_sem, w1_sem, w2_sem, halo_send, halo_recv, stat_send, stat_recv,
):
    me = lax.axis_index("tile")
    cap, rows, cols, c_in = feat.shape
    c_out = hid.shape[3]
    frames = cap + 2
    owners, videos = owner_ref.shape[0], video_ref.shape[0]
    cells = rows * cols
    height = rows * STRIPS
    vpad = st1.shape[0]

    def peer(by):
        return lax.rem(me + (by % n), n)

    barrier = pltpu.get_barrier_semaphore()

    def greet(d, carry):
        pl.semaphore_signal(barrier, inc=1, device_id={"tile": lax.rem(me + d, n)}, device_id_type=MESH)
        return carry

    load_feat = pltpu.make_async_copy(feat_hbm, feat, load_sem.at[0])
    small = [
        pltpu.make_async_copy(src, dst, small_sem.at[i])
        for i, (src, dst) in enumerate((
            (owner_hbm, owner_ref), (video_hbm, video_ref), (gain1_hbm, gain1), (shift1_hbm, shift1),
            (bias1_hbm, bias1), (gain2_hbm, gain2), (shift2_hbm, shift2), (bias2_hbm, bias2), (bias3_hbm, bias3)))
    ]
    load_w1 = [pltpu.make_async_copy(w1_hbm.at[k], w1.at[k], w1_sem.at[k]) for k in range(3)]
    load_w2 = [pltpu.make_async_copy(w2_hbm.at[k], w2.at[k], w2_sem.at[k]) for k in range(3)]
    load_skip = pltpu.make_async_copy(skip_hbm, skip, load_sem.at[1])
    lax.fori_loop(1, n, greet, 0)
    load_feat.start()
    for c in small:
        c.start()
    for c in load_w1:
        c.start()
    load_skip.start()
    for c in load_w2:
        c.start()

    position = lax.rem(me + STRIPS + STRIPS // 2, n)
    owner = position // STRIPS
    strip = position - owner * STRIPS
    small[0].wait()
    small[1].wait()
    first = jnp.int32(0)
    live = jnp.int32(0)
    for o in range(owners):
        count = owner_ref[o]
        first = first + jnp.where(o < owner, count, 0)
        live = live + jnp.where(o == owner, count, 0)
    tail = jnp.minimum(jnp.maximum(live - 2, 0), cap - 2)
    begins = []
    total = jnp.int32(0)
    for v in range(videos):
        begins.append(total)
        total = total + video_ref[v]
    which, started, lengths = [], [], []
    for f in range(frames):
        t = first + (f - 2)
        row, start, length = jnp.int32(-1), jnp.int32(0), jnp.int32(1)
        for v in range(videos):
            count = video_ref[v]
            hit = (t >= begins[v]) & (t < begins[v] + count)
            row = jnp.where(hit, v, row)
            start = jnp.where(hit, begins[v], start)
            length = jnp.where(hit, count, length)
        which.append(row)
        started.append(start)
        lengths.append(length)

    def halo_copies(stage, source, last, prior, up, down):
        moves = (
            (source.at[:, rows - 1], up.at[pl.ds(2, cap)], 1),
            (source.at[:, 0], down.at[pl.ds(2, cap)], -1),
            (last.at[:, rows - 1], up.at[pl.ds(0, 2)], STRIPS + 1),
            (last.at[:, 0], down.at[pl.ds(0, 2)], STRIPS - 1),
            (last, prior, STRIPS),
        )
        return [
            pltpu.make_async_remote_copy(
                src_ref=src, dst_ref=dst, send_sem=halo_send.at[stage, i], recv_sem=halo_recv.at[stage, i],
                device_id={"tile": peer(by)}, device_id_type=MESH)
            for i, (src, dst, by) in enumerate(moves)
        ]

    def stat_copy(stage, d, st, gath):
        return pltpu.make_async_remote_copy(
            src_ref=st, dst_ref=gath.at[d], send_sem=stat_send.at[stage, d], recv_sem=stat_recv.at[stage, d],
            device_id={"tile": lax.rem(me + d, n)}, device_id_type=MESH)

    def send_stats(stage, st, gath):
        def one(d, carry):
            stat_copy(stage, d, st, gath).start()
            return carry
        lax.fori_loop(1, n, one, 0)

    def wait_stats(stage, st, gath):
        def one(d, carry):
            stat_copy(stage, d, st, gath).wait()
            return carry
        lax.fori_loop(1, n, one, 0)

    row_ids = lax.broadcasted_iota(jnp.int32, (vpad, LANES), 0)

    def local_stats(values, channels):
        sums, squares = [], []
        for j in range(cap):
            x = values(j)
            sums.append(jnp.sum(x, axis=0, keepdims=True))
            squares.append(jnp.sum(x * x, axis=0, keepdims=True))
        pad = [jnp.zeros((8 - cap, channels), F32)] if cap < 8 else []
        s = jnp.concatenate(sums + pad, axis=0)
        q = jnp.concatenate(squares + pad, axis=0)
        grouped = jnp.dot(s, spread(channels, 0, False), precision=HIGHEST, preferred_element_type=F32)
        grouped = grouped + jnp.dot(
            q, spread(channels, GROUPS_N, False), precision=HIGHEST, preferred_element_type=F32)
        table = jnp.zeros((vpad, LANES), F32)
        for j in range(cap):
            target = jnp.where(j < live, which[j + 2], -1)
            table = table + jnp.where(row_ids == target, grouped[j:j + 1, :], 0.0)
        return table

    def tables(st, gath, channels, gain, shift):
        totals = st[...]
        for d in range(1, n):
            totals = totals + gath[d]
        ids = lax.broadcasted_iota(jnp.int32, (8, LANES), 0)
        picked = jnp.zeros((8, LANES), F32)
        counts = jnp.ones((8, LANES), F32)
        for f in range(frames):
            mine = jnp.sum(jnp.where(row_ids == which[f], totals, 0.0), axis=0, keepdims=True)
            picked = jnp.where(ids == f, mine, picked)
            size = (lengths[f] * (height * cols * (channels // GROUPS_N))).astype(F32)
            counts = jnp.where(ids == f, size, counts)
        average = picked / counts
        mean = jnp.dot(average, spread(channels, 0, True), precision=HIGHEST, preferred_element_type=F32)
        square = jnp.dot(average, spread(channels, GROUPS_N, True), precision=HIGHEST, preferred_element_type=F32)
        inverse = lax.rsqrt(jnp.maximum(square - mean * mean, 0.0) + EPS)
        return mean, inverse * gain[...].reshape(1, channels), shift[...].reshape(1, channels)

    def activate(x, f, table):
        mean, scale, offset = table
        u = (x.astype(F32) - mean[f:f + 1]) * scale[f:f + 1] + offset
        return (u * (0.5 + 0.5 * jnp.tanh(0.5 * u))).astype(BF16)

    def fill(act, span, own, prior, up, down, table):
        for f in span:
            for r in range(rows):
                x = prior[f, r] if f < 2 else own[f - 2, r]
                act[f, r + 1] = activate(x, f, table)
            top = activate(up[f], f, table)
            act[f, 0] = jnp.where(strip == 0, act[f, 1], top)
            low = activate(down[f], f, table)
            act[f, rows + 1] = jnp.where(strip == STRIPS - 1, act[f, rows], low)

    def convolve(act, w, slots, channels):
        at = pl.ds(slots[0] * cells, len(slots) * cells)

        def step(q, carry):
            lhs, rhs = [], []
            for k in range(3):
                frame = [
                    jnp.minimum(jnp.maximum(j + k, started[j + 2] - first + 2), frames - 1) for j in slots
                ]
                for i in range(3):
                    lhs.append(jnp.concatenate(
                        [act[f, i:i + rows].reshape(cells, channels) for f in frame], axis=0))
                    rhs.append(w[k, i, q])
            acc[q, at] = jnp.dot(
                jnp.concatenate(lhs, axis=1), jnp.concatenate(rhs, axis=0), preferred_element_type=F32)
            return carry

        lax.fori_loop(0, 3, step, 0)

    def joined(j):
        at = pl.ds(j * cells, cells)
        low, mid, high = acc[0, at], acc[1, at], acc[2, at]
        col = lax.rem(lax.broadcasted_iota(jnp.int32, low.shape, 0), cols)
        low = jnp.where(col == 0, low, pltpu.roll(low, 1, 0))
        high = jnp.where(col == cols - 1, high, pltpu.roll(high, cells - 1, 0))
        return low + mid + high

    load_feat.wait()
    last1[...] = feat[pl.ds(tail, 2)]
    st1[...] = local_stats(lambda j: feat[j].reshape(cells, c_in).astype(F32), c_in)
    pl.semaphore_wait(barrier, n - 1)
    halos = halo_copies(0, feat, last1, prior1, up1, down1)
    send_stats(0, st1, gath1)
    for c in halos:
        c.start()
    for c in small[2:]:
        c.wait()
    wait_stats(0, st1, gath1)
    table = tables(st1, gath1, c_in, gain1, shift1)
    for c in halos[:2]:
        c.wait()
    fill(act1, range(2, frames), feat, prior1, up1, down1, table)
    for c in load_w1:
        c.wait()
    convolve(act1, w1, range(2, cap), c_in)
    for c in halos[2:]:
        c.wait()
    fill(act1, range(2), feat, prior1, up1, down1, table)
    convolve(act1, w1, range(2), c_in)

    for j in range(cap):
        hid[j] = (joined(j) + bias1[...].reshape(1, c_out)).astype(BF16).reshape(rows, cols, c_out)
    last2[...] = hid[pl.ds(tail, 2)]
    st2[...] = local_stats(lambda j: hid[j].reshape(cells, c_out).astype(F32), c_out)
    halos = halo_copies(1, hid, last2, prior2, up2, down2)
    send_stats(1, st2, gath2)
    for c in halos:
        c.start()
    load_skip.wait()
    skipped[...] = jnp.dot(
        feat[...].reshape(cap * cells, c_in), skip[...], preferred_element_type=F32)
    wait_stats(1, st2, gath2)
    table = tables(st2, gath2, c_out, gain2, shift2)
    for c in halos[:2]:
        c.wait()
    fill(act2, range(2, frames), hid, prior2, up2, down2, table)
    for c in load_w2:
        c.wait()
    convolve(act2, w2, range(2, cap), c_out)
    for c in halos[2:]:
        c.wait()
    fill(act2, range(2), hid, prior2, up2, down2, table)
    convolve(act2, w2, range(2), c_out)
    extra = bias2[...].reshape(1, c_out) + bias3[...].reshape(1, c_out)
    for j in range(cap):
        value = joined(j) + skipped[pl.ds(j * cells, cells)] + extra
        value = jnp.where(j < live, value, 0.0)
        out_ref[j] = value.astype(BF16).reshape(rows, cols, c_out)


def on_device(n, features, owner_frames, video_frames, gain1, shift1, w1, bias1, gain2, shift2, w2, bias2, skip, bias3):
    cap, rows, cols, c_in = features.shape
    c_out = w1.shape[4]
    vpad = -(-video_frames.shape[0] // 8) * 8
    frames = cap + 2
    cells = rows * cols

    def buffers(channels):
        return [
            pltpu.VMEM((2, rows, cols, channels), BF16),
            pltpu.VMEM((2, rows, cols, channels), BF16),
            pltpu.VMEM((frames, cols, channels), BF16),
            pltpu.VMEM((frames, cols, channels), BF16),
            pltpu.VMEM((frames, rows + 2, cols, channels), BF16),
            pltpu.VMEM((vpad, LANES), F32),
            pltpu.VMEM((n, vpad, LANES), F32),
        ]

    hbm, vmem = (pl.BlockSpec(memory_space=s) for s in (pl.ANY, pltpu.VMEM))
    return pl.pallas_call(
        functools.partial(kernel, n),
        out_shape=pltpu.VMEM((cap, rows, cols, c_out), BF16),
        in_specs=[hbm] * 13,
        out_specs=vmem,
        scratch_shapes=[
            pltpu.SMEM(owner_frames.shape, jnp.int32),
            pltpu.SMEM(video_frames.shape, jnp.int32),
            *[pltpu.VMEM(p.shape, F32) for p in (gain1, shift1, bias1, gain2, shift2, bias2, bias3)],
            pltpu.VMEM(features.shape, BF16),
            pltpu.VMEM(w1.shape, BF16),
            pltpu.VMEM(w2.shape, BF16),
            pltpu.VMEM(skip.shape, BF16),
            *buffers(c_in),
            pltpu.VMEM((cap, rows, cols, c_out), BF16),
            *buffers(c_out),
            pltpu.VMEM((3, cap * cells, c_out), F32),
            pltpu.VMEM((cap * cells, c_out), F32),
            pltpu.SemaphoreType.DMA((2,)),
            pltpu.SemaphoreType.DMA((9,)),
            pltpu.SemaphoreType.DMA((3,)),
            pltpu.SemaphoreType.DMA((3,)),
            pltpu.SemaphoreType.DMA((2, 5)),
            pltpu.SemaphoreType.DMA((2, 5)),
            pltpu.SemaphoreType.DMA((2, n)),
            pltpu.SemaphoreType.DMA((2, n)),
        ],
        compiler_params=pltpu.CompilerParams(
            collective_id=0, has_side_effects=True, vmem_limit_bytes=60 * 1024 * 1024),
    )(features, owner_frames, video_frames, gain1, shift1, w1, bias1, gain2, shift2, w2, bias2, skip, bias3)


def solution(mesh):
    split = P(("groups", "tile"), None, None, None)
    placed = (split, P("groups"), P("groups")) + (P(),) * 10
    return jax.shard_map(
        functools.partial(on_device, mesh.shape["tile"]),
        mesh=mesh,
        in_specs=placed,
        out_specs=split,
        check_vma=False,
    )
```

```python
import functools

import jax
import jax.numpy as jnp
from jax import lax
from jax.experimental import pallas as pl
from jax.experimental.pallas import tpu as pltpu
from jax.sharding import PartitionSpec as P

GROUPS_N = 32
STRIPS = 4
LANES = 128
EPS = 1e-06
HIGHEST = lax.Precision.HIGHEST
MESH = pl.DeviceIdType.MESH
F32 = jnp.float32
BF16 = jnp.bfloat16


def spread(channels, offset, transposed):
    width = channels // GROUPS_N
    shape = (LANES, channels) if transposed else (channels, LANES)
    chan = lax.broadcasted_iota(jnp.int32, shape, 1 if transposed else 0)
    lane = (lax.broadcasted_iota(jnp.int32, shape, 0 if transposed else 1) - offset) * width
    return jnp.where((chan >= lane) & (chan < lane + width), 1.0, 0.0).astype(F32)


def kernel(
    n,
    feat_hbm, owner_hbm, video_hbm, gain1_hbm, shift1_hbm, w1_hbm, bias1_hbm, gain2_hbm, shift2_hbm, w2_hbm, bias2_hbm,
    skip_hbm, bias3_hbm,
    out_ref,
    owner_ref, video_ref, gain1, shift1, bias1, gain2, shift2, bias2, bias3,
    feat, w1, w2, skip,
    last1, prior1, up1, down1, act1, st1, gath1,
    hid, last2, prior2, up2, down2, act2, st2, gath2,
    acc, skipped,
    load_sem, small_sem, w1_sem, w2_sem, halo_send, halo_recv, stat_send, stat_recv,
):
    me = lax.axis_index("tile")
    cap, rows, cols, c_in = feat.shape
    c_out = hid.shape[3]
    frames = cap + 2
    owners, videos = owner_ref.shape[0], video_ref.shape[0]
    cells = rows * cols
    height = rows * STRIPS
    vpad = st1.shape[0]

    def peer(by):
        return lax.rem(me + (by % n), n)

    barrier = pltpu.get_barrier_semaphore()

    def greet(d, carry):
        pl.semaphore_signal(barrier, inc=1, device_id={"tile": lax.rem(me + d, n)}, device_id_type=MESH)
        return carry

    load_feat = pltpu.make_async_copy(feat_hbm, feat, load_sem.at[0])
    small = [
        pltpu.make_async_copy(src, dst, small_sem.at[i])
        for i, (src, dst) in enumerate((
            (owner_hbm, owner_ref), (video_hbm, video_ref), (gain1_hbm, gain1), (shift1_hbm, shift1),
            (bias1_hbm, bias1), (gain2_hbm, gain2), (shift2_hbm, shift2), (bias2_hbm, bias2), (bias3_hbm, bias3)))
    ]
    load_w1 = [pltpu.make_async_copy(w1_hbm.at[k], w1.at[k], w1_sem.at[k]) for k in range(3)]
    load_w2 = [pltpu.make_async_copy(w2_hbm.at[k], w2.at[k], w2_sem.at[k]) for k in range(3)]
    load_skip = pltpu.make_async_copy(skip_hbm, skip, load_sem.at[1])
    lax.fori_loop(1, n, greet, 0)
    load_feat.start()
    for c in small:
        c.start()
    for c in load_w1:
        c.start()
    load_skip.start()
    for c in load_w2:
        c.start()

    position = lax.rem(me + STRIPS + STRIPS // 2, n)
    owner = position // STRIPS
    strip = position - owner * STRIPS
    small[0].wait()
    small[1].wait()
    first = jnp.int32(0)
    live = jnp.int32(0)
    for o in range(owners):
        count = owner_ref[o]
        first = first + jnp.where(o < owner, count, 0)
        live = live + jnp.where(o == owner, count, 0)
    tail = jnp.minimum(jnp.maximum(live - 2, 0), cap - 2)
    begins = []
    total = jnp.int32(0)
    for v in range(videos):
        begins.append(total)
        total = total + video_ref[v]
    which, started, lengths = [], [], []
    for f in range(frames):
        t = first + (f - 2)
        row, start, length = jnp.int32(-1), jnp.int32(0), jnp.int32(1)
        for v in range(videos):
            count = video_ref[v]
            hit = (t >= begins[v]) & (t < begins[v] + count)
            row = jnp.where(hit, v, row)
            start = jnp.where(hit, begins[v], start)
            length = jnp.where(hit, count, length)
        which.append(row)
        started.append(start)
        lengths.append(length)

    def halo_copies(stage, source, last, prior, up, down):
        moves = (
            (source.at[:, rows - 1], up.at[pl.ds(2, cap)], 1),
            (source.at[:, 0], down.at[pl.ds(2, cap)], -1),
            (last.at[:, rows - 1], up.at[pl.ds(0, 2)], STRIPS + 1),
            (last.at[:, 0], down.at[pl.ds(0, 2)], STRIPS - 1),
            (last, prior, STRIPS),
        )
        return [
            pltpu.make_async_remote_copy(
                src_ref=src, dst_ref=dst, send_sem=halo_send.at[stage, i], recv_sem=halo_recv.at[stage, i],
                device_id={"tile": peer(by)}, device_id_type=MESH)
            for i, (src, dst, by) in enumerate(moves)
        ]

    above, below = strip > 0, strip < STRIPS - 1
    earlier, later = owner > 0, owner < n // STRIPS - 1
    sends = (below, above, below & later, above & later, later)
    takes = (above, below, above & earlier, below & earlier, earlier)

    def start_halos(halos):
        for c, sent in zip(halos, sends):
            pl.when(sent)(c.start)

    def wait_halos(halos, span):
        for i in span:
            pl.when(sends[i])(halos[i].wait_send)
            pl.when(takes[i])(halos[i].wait_recv)

    def stat_copy(stage, d, st, gath):
        return pltpu.make_async_remote_copy(
            src_ref=st, dst_ref=gath.at[d], send_sem=stat_send.at[stage, d], recv_sem=stat_recv.at[stage, d],
            device_id={"tile": lax.rem(me + d, n)}, device_id_type=MESH)

    def send_stats(stage, st, gath):
        def one(d, carry):
            stat_copy(stage, d, st, gath).start()
            return carry
        lax.fori_loop(1, n, one, 0)

    def wait_stats(stage, st, gath):
        def one(d, carry):
            stat_copy(stage, d, st, gath).wait()
            return carry
        lax.fori_loop(1, n, one, 0)

    row_ids = lax.broadcasted_iota(jnp.int32, (vpad, LANES), 0)

    def local_stats(values, channels):
        sums, squares = [], []
        for j in range(cap):
            x = values(j)
            sums.append(jnp.sum(x, axis=0, keepdims=True))
            squares.append(jnp.sum(x * x, axis=0, keepdims=True))
        pad = [jnp.zeros((8 - cap, channels), F32)] if cap < 8 else []
        s = jnp.concatenate(sums + pad, axis=0)
        q = jnp.concatenate(squares + pad, axis=0)
        grouped = jnp.dot(s, spread(channels, 0, False), precision=HIGHEST, preferred_element_type=F32)
        grouped = grouped + jnp.dot(
            q, spread(channels, GROUPS_N, False), precision=HIGHEST, preferred_element_type=F32)
        table = jnp.zeros((vpad, LANES), F32)
        for j in range(cap):
            target = jnp.where(j < live, which[j + 2], -1)
            table = table + jnp.where(row_ids == target, grouped[j:j + 1, :], 0.0)
        return table

    def tables(st, gath, channels, gain, shift):
        totals = st[...]
        for d in range(1, n):
            totals = totals + gath[d]
        ids = lax.broadcasted_iota(jnp.int32, (8, LANES), 0)
        picked = jnp.zeros((8, LANES), F32)
        counts = jnp.ones((8, LANES), F32)
        for f in range(frames):
            mine = jnp.sum(jnp.where(row_ids == which[f], totals, 0.0), axis=0, keepdims=True)
            picked = jnp.where(ids == f, mine, picked)
            size = (lengths[f] * (height * cols * (channels // GROUPS_N))).astype(F32)
            counts = jnp.where(ids == f, size, counts)
        average = picked / counts
        mean = jnp.dot(average, spread(channels, 0, True), precision=HIGHEST, preferred_element_type=F32)
        square = jnp.dot(average, spread(channels, GROUPS_N, True), precision=HIGHEST, preferred_element_type=F32)
        inverse = lax.rsqrt(jnp.maximum(square - mean * mean, 0.0) + EPS)
        return mean, inverse * gain[...].reshape(1, channels), shift[...].reshape(1, channels)

    def activate(x, f, table):
        mean, scale, offset = table
        u = (x.astype(F32) - mean[f:f + 1]) * scale[f:f + 1] + offset
        return (u * (0.5 + 0.5 * jnp.tanh(0.5 * u))).astype(BF16)

    def fill(act, span, own, prior, up, down, table):
        for f in span:
            for r in range(rows):
                x = prior[f, r] if f < 2 else own[f - 2, r]
                act[f, r + 1] = activate(x, f, table)
            top = activate(up[f], f, table)
            act[f, 0] = jnp.where(strip == 0, act[f, 1], top)
            low = activate(down[f], f, table)
            act[f, rows + 1] = jnp.where(strip == STRIPS - 1, act[f, rows], low)

    def convolve(act, w, slots, taps, channels, onto=False):
        at = pl.ds(slots[0] * cells, len(slots) * cells)

        def step(q, carry):
            lhs, rhs = [], []
            for k in taps:
                frame = [
                    jnp.minimum(jnp.maximum(j + k, started[j + 2] - first + 2), frames - 1) for j in slots
                ]
                for i in range(3):
                    lhs.append(jnp.concatenate(
                        [act[f, i:i + rows].reshape(cells, channels) for f in frame], axis=0))
                    rhs.append(w[k, i, q])
            product = jnp.dot(
                jnp.concatenate(lhs, axis=1), jnp.concatenate(rhs, axis=0), preferred_element_type=F32)
            acc[q, at] = acc[q, at] + product if onto else product
            return carry

        lax.fori_loop(0, 3, step, 0)

    def joined(j):
        at = pl.ds(j * cells, cells)
        low, mid, high = acc[0, at], acc[1, at], acc[2, at]
        col = lax.rem(lax.broadcasted_iota(jnp.int32, low.shape, 0), cols)
        low = jnp.where(col == 0, low, pltpu.roll(low, 1, 0))
        high = jnp.where(col == cols - 1, high, pltpu.roll(high, cells - 1, 0))
        return low + mid + high

    load_feat.wait()
    last1[...] = feat[pl.ds(tail, 2)]
    st1[...] = local_stats(lambda j: feat[j].reshape(cells, c_in).astype(F32), c_in)
    pl.semaphore_wait(barrier, n - 1)
    halos = halo_copies(0, feat, last1, prior1, up1, down1)
    send_stats(0, st1, gath1)
    start_halos(halos)
    for c in small[2:]:
        c.wait()
    wait_stats(0, st1, gath1)
    table = tables(st1, gath1, c_in, gain1, shift1)
    wait_halos(halos, range(2))
    fill(act1, range(2, frames), feat, prior1, up1, down1, table)
    for c in load_w1:
        c.wait()
    convolve(act1, w1, range(2, cap), range(3), c_in)
    convolve(act1, w1, range(2), range(2, 3), c_in)
    wait_halos(halos, range(2, 5))
    fill(act1, range(2), feat, prior1, up1, down1, table)
    convolve(act1, w1, range(2), range(2), c_in, True)

    for j in range(cap):
        hid[j] = (joined(j) + bias1[...].reshape(1, c_out)).astype(BF16).reshape(rows, cols, c_out)
    last2[...] = hid[pl.ds(tail, 2)]
    st2[...] = local_stats(lambda j: hid[j].reshape(cells, c_out).astype(F32), c_out)
    halos = halo_copies(1, hid, last2, prior2, up2, down2)
    send_stats(1, st2, gath2)
    start_halos(halos)
    load_skip.wait()
    skipped[...] = jnp.dot(
        feat[...].reshape(cap * cells, c_in), skip[...], preferred_element_type=F32)
    wait_stats(1, st2, gath2)
    table = tables(st2, gath2, c_out, gain2, shift2)
    wait_halos(halos, range(2))
    fill(act2, range(2, frames), hid, prior2, up2, down2, table)
    for c in load_w2:
        c.wait()
    convolve(act2, w2, range(2, cap), range(3), c_out)
    convolve(act2, w2, range(2), range(2, 3), c_out)
    wait_halos(halos, range(2, 5))
    fill(act2, range(2), hid, prior2, up2, down2, table)
    convolve(act2, w2, range(2), range(2), c_out, True)
    extra = bias2[...].reshape(1, c_out) + bias3[...].reshape(1, c_out)
    for j in range(cap):
        value = joined(j) + skipped[pl.ds(j * cells, cells)] + extra
        value = jnp.where(j < live, value, 0.0)
        out_ref[j] = value.astype(BF16).reshape(rows, cols, c_out)


def on_device(n, features, owner_frames, video_frames, gain1, shift1, w1, bias1, gain2, shift2, w2, bias2, skip, bias3):
    cap, rows, cols, c_in = features.shape
    c_out = w1.shape[4]
    vpad = video_frames.shape[0]
    frames = cap + 2
    cells = rows * cols

    def buffers(channels):
        return [
            pltpu.VMEM((2, rows, cols, channels), BF16),
            pltpu.VMEM((2, rows, cols, channels), BF16),
            pltpu.VMEM((frames, cols, channels), BF16),
            pltpu.VMEM((frames, cols, channels), BF16),
            pltpu.VMEM((frames, rows + 2, cols, channels), BF16),
            pltpu.VMEM((vpad, LANES), F32),
            pltpu.VMEM((n, vpad, LANES), F32),
        ]

    hbm, vmem = (pl.BlockSpec(memory_space=s) for s in (pl.ANY, pltpu.VMEM))
    return pl.pallas_call(
        functools.partial(kernel, n),
        out_shape=pltpu.VMEM((cap, rows, cols, c_out), BF16),
        in_specs=[hbm] * 13,
        out_specs=vmem,
        scratch_shapes=[
            pltpu.SMEM(owner_frames.shape, jnp.int32),
            pltpu.SMEM(video_frames.shape, jnp.int32),
            *[pltpu.VMEM(p.shape, F32) for p in (gain1, shift1, bias1, gain2, shift2, bias2, bias3)],
            pltpu.VMEM(features.shape, BF16),
            pltpu.VMEM(w1.shape, BF16),
            pltpu.VMEM(w2.shape, BF16),
            pltpu.VMEM(skip.shape, BF16),
            *buffers(c_in),
            pltpu.VMEM((cap, rows, cols, c_out), BF16),
            *buffers(c_out),
            pltpu.VMEM((3, cap * cells, c_out), F32),
            pltpu.VMEM((cap * cells, c_out), F32),
            pltpu.SemaphoreType.DMA((2,)),
            pltpu.SemaphoreType.DMA((9,)),
            pltpu.SemaphoreType.DMA((3,)),
            pltpu.SemaphoreType.DMA((3,)),
            pltpu.SemaphoreType.DMA((2, 5)),
            pltpu.SemaphoreType.DMA((2, 5)),
            pltpu.SemaphoreType.DMA((2, n)),
            pltpu.SemaphoreType.DMA((2, n)),
        ],
        compiler_params=pltpu.CompilerParams(
            collective_id=0, has_side_effects=True, vmem_limit_bytes=60 * 1024 * 1024),
    )(features, owner_frames, video_frames, gain1, shift1, w1, bias1, gain2, shift2, w2, bias2, skip, bias3)


def solution(mesh):
    split = P(("groups", "tile"), None, None, None)
    placed = (split, P("groups"), P("groups")) + (P(),) * 10
    return jax.shard_map(
        functools.partial(on_device, mesh.shape["tile"]),
        mesh=mesh,
        in_specs=placed,
        out_specs=split,
        check_vma=False,
    )
```
